128 devices in a mesh: ctx: 16 (over y_hi, z, core), head: 8 (over x, y_lo).
Axes of the slice: x: 4, y: 4 (y_hi: 2, y_lo: 2; y = y_hi * 2 + y_lo), z: 4, core: 2. Of those that a mesh axis runs over, the one named last changes fastest.
Arguments:
- query_states: bfloat16 [32768, 16, 128], P('ctx', 'head'), may hold values from -36 to 36, as said below
- key_states: bfloat16 [32768, 16, 128], P('ctx', 'head'), may hold values from -6 to 6
- value_states: bfloat16 [32768, 16, 128], P('ctx', 'head'), may hold values from -6 to 6
- block_pattern: int32 [16, 256, 256], P('head'), may hold values 0 or 1
- helper_distances: int32 [2], replicated, may hold values from 1 to 8, as said below
- out_weight: bfloat16 [16, 128, 4096], P('head'), may hold values from -0.125 to 0.125
Outputs:
- layer_output: bfloat16 [32768, 4096], P(('ctx', 'head'))
The draws below stay inside these ranges and needn't reach their ends.
Inputs may be any that keep to these rules, and one draw needn't show every extreme that they name: `query_states`: Queries; some rows may be large multiples of key rows. `helper_distances`: the two distances differ, and one of them is always 8.
All inputs are finite; a program needn't handle non-finite values. No bound on the sum of `block_pattern` on one device may be relied on, other than what follows from the above.
Results may differ from the reference program's by a relative error of at most 0.015.
Values may be sent and summed in bfloat16 or wider, within the bound.
A program may use at most 128 MiB of HBM per device.

```python
import jax
import jax.numpy as jnp
from jax import lax

D = 4096
HEADS = 16
HEAD_DIM = 128
BLOCK = 128
ROUNDS = 2
CTX_DEV = 2048
SHARDS = 16
SEQ = 32768
NB = 256
N_HEAD = 8


def draw_pair(key):
    full_shape = (SEQ, HEADS, HEAD_DIM)
    query_key = jax.random.fold_in(key, 7001)
    state_key = jax.random.fold_in(key, 7002)
    queries = jnp.clip(jax.random.normal(query_key, full_shape, jnp.float32), -6.0, 6.0)
    states = jnp.clip(jax.random.normal(state_key, full_shape, jnp.float32), -6.0, 6.0)
    return (queries, states)


def draw_query_states(key, part):
    return draw_pair(key)[0].astype(jnp.bfloat16)


def draw_key_states(key, part):
    return draw_pair(key)[1].astype(jnp.bfloat16)


def draw_helper_distances(key, part):
    half_way = SHARDS // 2
    other_hop = jax.random.randint(jax.random.fold_in(key, 9101), (), 1, half_way)
    flip_bit = jax.random.randint(jax.random.fold_in(key, 9102), (), 0, 2)
    first_hop = jnp.where(flip_bit == 1, half_way, other_hop)
    second_hop = jnp.where(flip_bit == 1, other_hop, half_way)
    return jnp.stack([first_hop, second_hop]).astype(jnp.int32)


def plant(drawn, rng, least, top_value):
    longest = drawn.shape.index(max(drawn.shape))
    spots = []
    for shift in (0, 1):
        where = [jax.random.randint(jax.random.fold_in(rng, axis), (), 0, length) for axis, length in enumerate(drawn.shape)]
        where[longest] = (where[longest] + shift) % drawn.shape[longest]
        spots.append(tuple(where))
    return drawn.at[spots[0]].set(least).at[spots[1]].set(top_value)


def levels(key, dims, cuts, smallest, largest):
    level, own = 1.0, jax.random.fold_in(key, 6)
    for position, blocks in cuts:
        heights = jnp.exp(jax.random.uniform(jax.random.fold_in(own, position), (blocks,), jnp.float32, smallest / len(cuts), largest / len(cuts)))
        level = level * jnp.repeat(heights, dims[position] // blocks).reshape([-1 if axis == position else 1 for axis in range(len(dims))])
    return level


def centred(rng, extent, scale, most, split=(), kind=jnp.bfloat16):
    values = jax.random.normal(rng, extent, jnp.float32) * scale
    if len(split) > 0:
        values = levels(rng, extent, split, -0.22, 0.18) * values
    return jnp.clip(values, min=-most, max=most).astype(kind)


def setup_inputs(seed: int = 0) -> dict:
    key_of = jax.random.split(jax.random.key(seed), 7)
    query_states = draw_query_states(jax.random.fold_in(key_of[6], 71), 0)
    key_states = draw_key_states(jax.random.fold_in(key_of[6], 71), 0)
    value_states = centred(key_of[2], (SEQ, HEADS, HEAD_DIM), 1.0, 6.0, ((0, 16), (1, 8)))
    block_pattern = plant((jax.random.randint(key_of[3], (HEADS, NB, NB), 0, 5) < 2).astype(jnp.int32), jax.random.fold_in(key_of[3], 1), 0, 1)
    helper_distances = draw_helper_distances(jax.random.fold_in(key_of[6], 71), 0)
    out_weight = centred(key_of[5], (HEADS, HEAD_DIM, D), (HEADS * HEAD_DIM) ** -0.5, 0.125, ((0, 8),))
    return {"query_states": query_states, "key_states": key_states, "value_states": value_states, "block_pattern": block_pattern, "helper_distances": helper_distances, "out_weight": out_weight}


NEG_FILL = -1.0e30


def attend_source(query_part, key_part, value_part, pattern_rows, is_local):
    row_count = query_part.shape[0]
    key_count = key_part.shape[0]
    row_step = min(512, row_count)
    score_scale = query_part.shape[2] ** -0.5
    key_place = jnp.arange(key_count, dtype=jnp.int32)

    def one_block(block_number):
        first_row = (block_number * row_step).astype(jnp.int32)
        query_rows = lax.dynamic_slice_in_dim(query_part, first_row, row_step, 0)
        pattern_part = lax.dynamic_slice_in_dim(pattern_rows, (first_row // BLOCK).astype(jnp.int32), row_step // BLOCK, 1)
        allowed = jnp.repeat(jnp.repeat(pattern_part > 0, BLOCK, axis=1), BLOCK, axis=2)
        if is_local:
            query_place = first_row + jnp.arange(row_step, dtype=jnp.int32)
            query_block = query_place // BLOCK
            key_block = key_place // BLOCK
            earlier = key_block[None, :] < query_block[:, None]
            same_block = (key_block[None, :] == query_block[:, None]) & (key_place[None, :] <= query_place[:, None])
            allowed = (allowed & earlier[None]) | same_block[None]
        scores = jnp.einsum("qhe,khe->hqk", query_rows.astype(jnp.float32), key_part.astype(jnp.float32),
                            precision=lax.Precision.HIGHEST) * score_scale
        masked = jnp.where(allowed, scores, NEG_FILL)
        row_peak = jnp.max(masked, axis=2)
        weights = jnp.where(allowed, jnp.exp(masked - row_peak[:, :, None]), 0.0)
        row_total = jnp.sum(weights, axis=2)
        rounded = lax.optimization_barrier(weights.astype(jnp.bfloat16)).astype(jnp.float32)
        numerator = jnp.einsum("hqk,khe->qhe", rounded, value_part.astype(jnp.float32),
                               precision=lax.Precision.HIGHEST)
        return numerator, row_peak.T, row_total.T

    numerator, row_peak, row_total = lax.map(one_block, jnp.arange(row_count // row_step, dtype=jnp.int32))
    heads_here = query_part.shape[1]
    return (numerator.reshape(row_count, heads_here, query_part.shape[2]),
            row_peak.reshape(row_count, heads_here), row_total.reshape(row_count, heads_here))


def keep_valid(piece, is_valid):
    numerator, row_peak, row_total = piece
    return (jnp.where(is_valid, numerator, 0.0), jnp.where(is_valid, row_peak, NEG_FILL),
            jnp.where(is_valid, row_total, 0.0))


def combine_sources(pieces):
    peak_score = pieces[0][1]
    for piece in pieces[1:]:
        peak_score = jnp.maximum(peak_score, piece[1])
    numerator_sum = jnp.zeros_like(pieces[0][0])
    denominator = jnp.zeros_like(pieces[0][1])
    for numerator, row_peak, row_total in pieces:
        factor = jnp.exp(row_peak - peak_score)
        numerator_sum = numerator_sum + factor[:, :, None] * numerator
        denominator = denominator + factor * row_total
    return (numerator_sum / denominator[:, :, None]).astype(jnp.bfloat16)


def reference(query_states, key_states, value_states, block_pattern, helper_distances, out_weight):
    per_shard = CTX_DEV // BLOCK

    def pattern_rows(query_shard, key_shard):
        starts = (jnp.zeros((), jnp.int32), (query_shard * per_shard).astype(jnp.int32),
                  (key_shard * per_shard).astype(jnp.int32))
        return lax.dynamic_slice(block_pattern, starts, (HEADS, per_shard, per_shard))

    def one_shard(my_shard):
        start_row = (my_shard * CTX_DEV).astype(jnp.int32)
        query_part = lax.dynamic_slice_in_dim(query_states, start_row, CTX_DEV, 0)
        key_part = lax.dynamic_slice_in_dim(key_states, start_row, CTX_DEV, 0)
        value_part = lax.dynamic_slice_in_dim(value_states, start_row, CTX_DEV, 0)
        pieces = [attend_source(query_part, key_part, value_part, pattern_rows(my_shard, my_shard), True)]
        for round_number in range(ROUNDS):
            source = my_shard - helper_distances[round_number].astype(jnp.int32)
            safe_source = jnp.maximum(source, 0).astype(jnp.int32)
            far_start = (safe_source * CTX_DEV).astype(jnp.int32)
            far_keys = lax.dynamic_slice_in_dim(key_states, far_start, CTX_DEV, 0)
            far_values = lax.dynamic_slice_in_dim(value_states, far_start, CTX_DEV, 0)
            piece = attend_source(query_part, far_keys, far_values, pattern_rows(my_shard, safe_source), False)
            pieces.append(keep_valid(piece, source >= 0))
        return combine_sources(pieces)

    attended = lax.map(one_shard, jnp.arange(SHARDS, dtype=jnp.int32))
    flattened = attended.reshape(SEQ, HEADS * HEAD_DIM)
    weight_rows = out_weight.reshape(HEADS * HEAD_DIM, D)
    group_width = (HEADS // N_HEAD) * HEAD_DIM
    output_sum = jnp.zeros((SEQ, D), jnp.float32)
    for group in range(N_HEAD):
        partial_value = jnp.dot(flattened[:, group * group_width:(group + 1) * group_width],
                          weight_rows[group * group_width:(group + 1) * group_width],
                          preferred_element_type=jnp.float32)
        partial_value = lax.optimization_barrier(partial_value.astype(jnp.bfloat16))
        output_sum = output_sum + partial_value.astype(jnp.float32)
    return output_sum.astype(jnp.bfloat16)
```

```python
import functools

import jax
import jax.numpy as jnp
from jax import lax
from jax.experimental import pallas as pl
from jax.experimental.pallas import tpu as pltpu
from jax.sharding import PartitionSpec as P

BLOCK = 128
HEAD_DIM = 128
NEG = -1e30
BIG = 1e30
SCALE = HEAD_DIM**-0.5 * 1.4426950408889634
FAR = 8
TILE = 256
BLOCKS_IN = TILE // BLOCK
STAT_ROWS = 16
OUT_ROWS = HEAD_DIM + STAT_ROWS
BF16 = jnp.bfloat16
F32 = jnp.float32
NT = (((1,), (1,)), ((), ()))
NN = (((1,), (0,)), ((), ()))
WHOLE = pl.BlockSpec(memory_space=pltpu.VMEM)
VMEM_LIMIT = 56 << 20


def cost(flops, bytes_moved):
    return pl.CostEstimate(flops=flops, bytes_accessed=bytes_moved, transcendentals=0)


def split_queries_kernel(x_ref, a_ref, b_ref, wide):
    rows = a_ref.shape[0]

    def step(i, carry):
        start = pl.multiple_of(i * 512, 512)
        half = pl.multiple_of(i * 256, 256)
        wide[...] = x_ref[pl.ds(start, 512), :].astype(F32)
        for h, out in enumerate((a_ref, b_ref)):
            out[pl.ds(half, 256), :] = wide[pl.ds(h, 256, stride=2), :].astype(BF16)
        return carry

    lax.fori_loop(0, rows // 256, step, 0)


def split_queries(x):
    rows = x.shape[0]
    out = jax.ShapeDtypeStruct((rows, HEAD_DIM), BF16)
    return pl.pallas_call(
        split_queries_kernel,
        in_specs=[WHOLE],
        out_specs=[WHOLE] * 2,
        out_shape=[out] * 2,
        scratch_shapes=[pltpu.VMEM((512, HEAD_DIM), F32)],
        cost_estimate=cost(0, 2 * x.size * 2),
        name="split_queries",
    )(x.reshape(rows * 2, HEAD_DIM))


def split_kv_kernel(k_ref, v_ref, ko_ref, vo_ref, wide_k, wide_v):
    rows = ko_ref.shape[1]

    def step(i, carry):
        start = pl.multiple_of(i * 512, 512)
        half = pl.multiple_of(i * 256, 256)
        wide_k[...] = k_ref[pl.ds(start, 512), :].astype(F32)
        wide_v[...] = v_ref[pl.ds(start, 512), :].astype(F32)
        for h in range(2):
            ko_ref[h, pl.ds(half, 256), :] = wide_k[pl.ds(h, 256, stride=2), :].astype(BF16)
            vo_ref[h, :, pl.ds(half, 256)] = wide_v[pl.ds(h, 256, stride=2), :].T.astype(BF16)
        return carry

    lax.fori_loop(0, rows // 256, step, 0)


def split_kv(k, v):
    rows = k.shape[0]
    return pl.pallas_call(
        split_kv_kernel,
        in_specs=[WHOLE] * 2,
        out_specs=[WHOLE] * 2,
        out_shape=[
            jax.ShapeDtypeStruct((2, rows, HEAD_DIM), BF16),
            jax.ShapeDtypeStruct((2, HEAD_DIM, rows), BF16),
        ],
        scratch_shapes=[pltpu.VMEM((512, HEAD_DIM), F32)] * 2,
        cost_estimate=cost(0, 4 * k.size * 2),
        name="split_kv",
    )(k.reshape(rows * 2, HEAD_DIM), v.reshape(rows * 2, HEAD_DIM))


def score_chunk(j, q, k_ref, h, mask_ref, off, s_ref, peak, diagonal):
    keys = slice(j * TILE, (j + 1) * TILE)
    s = lax.dot_general(k_ref[h, keys, :], q, NT, preferred_element_type=F32)
    if diagonal:
        parts = []
        place_k = lax.broadcasted_iota(jnp.int32, (BLOCK, TILE), 0)
        place_q = lax.broadcasted_iota(jnp.int32, (BLOCK, TILE), 1)
        for b in range(BLOCKS_IN):
            i = j * BLOCKS_IN + b
            row = mask_ref[h, i : i + 1, pl.ds(off, TILE)]
            same = (place_q >= b * BLOCK) & (place_q < (b + 1) * BLOCK)
            later = (place_q >= (b + 1) * BLOCK) & (row > 0)
            allowed = (same & (place_k + b * BLOCK <= place_q)) | later
            parts.append(jnp.where(allowed, s[b * BLOCK : (b + 1) * BLOCK], NEG))
        s = jnp.concatenate(parts, 0)
    s_ref[keys] = s
    for b in range(BLOCKS_IN):
        i = j * BLOCKS_IN + b
        block_peak = s[b * BLOCK : (b + 1) * BLOCK].reshape(BLOCK // 8, 8, TILE).max(0)
        if not diagonal:
            row = mask_ref[h, i : i + 1, pl.ds(off, TILE)]
            block_peak = jnp.where(row > 0, block_peak, NEG)
        peak = jnp.maximum(peak, block_peak)
    return peak


def value_chunk(j, peak, v_ref, h, mask_ref, off, s_ref, total, acc, diagonal):
    parts = []
    for b in range(BLOCKS_IN):
        i = j * BLOCKS_IN + b
        shift = peak
        if not diagonal:
            row = mask_ref[h, i : i + 1, pl.ds(off, TILE)]
            shift = jnp.where(row > 0, peak, BIG)
        p = jnp.exp2((s_ref[i * BLOCK : (i + 1) * BLOCK] - shift) * SCALE)
        total = total + p.reshape(BLOCK // 8, 8, TILE).sum(0)
        parts.append(p.astype(BF16))
    weights = jnp.concatenate(parts, 0)
    keys = slice(j * TILE, (j + 1) * TILE)
    return total, acc + lax.dot_general(v_ref[h, :, keys], weights, NN, preferred_element_type=F32)


def three_parts(x):
    first = x.astype(BF16)
    rest = x - first.astype(F32)
    second = rest.astype(BF16)
    return [first.astype(F32), second.astype(F32), rest - second.astype(F32)]


def finish(peak, total, acc):
    total = total.sum(0, keepdims=True)
    inverse = jnp.where(total > 0, 1.0 / jnp.where(total > 0, total, 1.0), 0.0)
    rows = three_parts(peak) + three_parts(total)
    rows.append(jnp.zeros((STAT_ROWS - 6, TILE), F32))
    return jnp.concatenate([acc * inverse] + rows, 0).astype(BF16)


def phase(first, second, q_ref, k_ref, v_ref, mask_ref, o_ref, peak_ref, s_first, s_second, chunks):
    if first is not None:
        h1, t1, n1 = first
        off1 = t1 * TILE if isinstance(t1, int) else pl.multiple_of(t1 * TILE, TILE)
        q = q_ref[h1, pl.ds(off1, TILE), :]
        peak1 = jnp.full((8, TILE), NEG, F32)
    if second is not None:
        h2, t2, n2 = second
        off2 = t2 * TILE if isinstance(t2, int) else pl.multiple_of(t2 * TILE, TILE)
        peak2 = peak_ref[...]
        total = jnp.zeros((8, TILE), F32)
        acc = jnp.zeros((HEAD_DIM, TILE), F32)
    local = chunks is None
    for j in range(max(n1 if first is not None else 0, n2 if second is not None else 0)):
        if first is not None and j < n1:
            peak1 = score_chunk(
                j, q, k_ref, h1, mask_ref, off1, s_first, peak1, local and j == n1 - 1
            )
        if second is not None and j < n2:
            total, acc = value_chunk(
                j, peak2, v_ref, h2, mask_ref, off2, s_second, total, acc, local and j == n2 - 1
            )
    if second is not None:
        o_ref[h2, :, pl.ds(off2, TILE)] = finish(peak2, total, acc)
    if first is not None:
        peak_ref[...] = peak1.max(0, keepdims=True)


def local_kernel(q0_ref, q1_ref, k_ref, v_ref, mask_ref, o_ref, s_a, s_b, peak_ref):
    tiles = q0_ref.shape[0] // TILE
    for h, q_ref in enumerate((q0_ref, q1_ref)):
        before = None
        for t in range(tiles + 1):
            now = (h, t, t + 1) if t < tiles else None
            sa, sb = (s_a, s_b) if t % 2 == 0 else (s_b, s_a)
            phase(
                now, before, SingleHead(q_ref), k_ref, v_ref, mask_ref, o_ref,
                peak_ref, sa, sb, None,
            )
            before = now


class SingleHead:
    def __init__(self, ref):
        self.ref = ref

    def __getitem__(self, index):
        return self.ref[index[1:]]


class SingleOut:
    def __init__(self, ref):
        self.ref = ref

    def __setitem__(self, index, value):
        self.ref[index[1:]] = value


def helper_kernel(q_ref, k_ref, v_ref, mask_ref, o_ref, s_a, s_b, peak_ref):
    tiles = q_ref.shape[0] // TILE
    chunks = k_ref.shape[1] // TILE
    rest = (SingleHead(q_ref), k_ref, v_ref, mask_ref, SingleOut(o_ref), peak_ref)
    peak_ref[...] = jnp.zeros_like(peak_ref)

    def step(i, carry):
        phase((0, 2 * i, chunks), (0, jnp.maximum(2 * i - 1, 0), chunks), *rest, s_a, s_b, chunks)
        phase((0, 2 * i + 1, chunks), (0, 2 * i, chunks), *rest, s_b, s_a, chunks)
        return carry

    lax.fori_loop(0, tiles // 2, step, 0)
    phase(None, (0, tiles - 1, chunks), *rest, s_a, s_b, chunks)


def attention_scratch(rows):
    return [
        pltpu.VMEM((rows, TILE), F32),
        pltpu.VMEM((rows, TILE), F32),
        pltpu.VMEM((1, TILE), F32),
    ]


def local_attention(q0, q1, k, v, mask):
    rows = q0.shape[0]
    return pl.pallas_call(
        local_kernel,
        in_specs=[WHOLE] * 5,
        out_specs=WHOLE,
        out_shape=jax.ShapeDtypeStruct((2, OUT_ROWS, rows), BF16),
        scratch_shapes=attention_scratch(rows),
        compiler_params=pltpu.CompilerParams(vmem_limit_bytes=VMEM_LIMIT),
        cost_estimate=cost(rows * rows * 512, 5 * rows * 512),
        name="local_attention",
    )(q0, q1, k, v, mask)


def helper_attention(h, q, k, v, mask):
    rows = q.shape[0]
    keys = k.shape[1]
    return pl.pallas_call(
        helper_kernel,
        grid=(1,),
        in_specs=[
            pl.BlockSpec((rows, HEAD_DIM), lambda i: (0, 0)),
            pl.BlockSpec((1, keys, HEAD_DIM), lambda i: (h, 0, 0)),
            pl.BlockSpec((1, HEAD_DIM, keys), lambda i: (h, 0, 0)),
            pl.BlockSpec((1, mask.shape[1], rows), lambda i: (h, 0, 0)),
        ],
        out_specs=pl.BlockSpec((OUT_ROWS, rows), lambda i: (0, 0)),
        out_shape=jax.ShapeDtypeStruct((OUT_ROWS, rows), BF16),
        scratch_shapes=attention_scratch(keys),
        compiler_params=pltpu.CompilerParams(vmem_limit_bytes=VMEM_LIMIT),
        cost_estimate=cost(rows * keys * 512, 5 * rows * 256),
        name="helper_attention",
    )(q, k, v, mask)


def allowed_rows(block_pattern, query_shard, key_shard, per_shard):
    starts = (jnp.zeros((), jnp.int32), query_shard * per_shard, key_shard * per_shard)
    part = lax.dynamic_slice(block_pattern, starts, (block_pattern.shape[0], per_shard, per_shard))
    part = jnp.transpose(part, (0, 2, 1)).astype(F32)
    return jnp.repeat(part, BLOCK, axis=2)


def merge_kernel(valid_ref, own_ref, a0_ref, a1_ref, b0_ref, b1_ref, out_ref):
    for h, others in enumerate(((a0_ref, b0_ref), (a1_ref, b1_ref))):
        pieces = []
        for r, part in enumerate([own_ref[h]] + [ref[...] for ref in others]):
            part = part.astype(F32)
            stats = part[HEAD_DIM:]
            peak = stats[0:1] + stats[1:2] + stats[2:3]
            total = stats[3:4] + stats[4:5] + stats[5:6]
            if r > 0:
                valid = valid_ref[r - 1] > 0
                peak = jnp.where(valid, peak, NEG)
                total = jnp.where(valid, total, 0.0)
            pieces.append((part[:HEAD_DIM], peak, total))
        top = jnp.maximum(jnp.maximum(pieces[0][1], pieces[1][1]), pieces[2][1])
        factors = [jnp.exp2((peak - top) * SCALE) * total for _, peak, total in pieces]
        inverse = 1.0 / (factors[0] + factors[1] + factors[2])
        mixed = sum(part * (factor * inverse) for (part, _, _), factor in zip(pieces, factors))
        out_ref[:, h * HEAD_DIM : (h + 1) * HEAD_DIM] = mixed.T.astype(BF16)


def merge(valid, own, far, near):
    rows = own.shape[2]
    single = pl.BlockSpec((OUT_ROWS, TILE), lambda i, v: (0, i))
    return pl.pallas_call(
        merge_kernel,
        grid_spec=pltpu.PrefetchScalarGridSpec(
            num_scalar_prefetch=1,
            grid=(rows // TILE,),
            in_specs=[pl.BlockSpec((2, OUT_ROWS, TILE), lambda i, v: (0, 0, i))] + [single] * 4,
            out_specs=pl.BlockSpec((None, TILE, 2 * HEAD_DIM), lambda i, v: (i, 0, 0)),
        ),
        out_shape=jax.ShapeDtypeStruct((rows // TILE, TILE, 2 * HEAD_DIM), BF16),
        cost_estimate=cost(rows * 2048, rows * 2048),
        name="merge",
    )(valid, own, *far, *near)


def project_kernel(order_ref, att_ref, own_ref, *refs):
    pieces, out_ref = refs[:-1], refs[-1]
    count = len(pieces) // 2
    i = pl.program_id(0)
    core = order_ref[count + 1]
    width = pieces[0].shape[2]
    half = out_ref.shape[1] // 2
    for side in range(2):
        where = core if side == 0 else 1 - core
        start = pl.multiple_of(where * half + i * width, width)
        acc = lax.dot_general(
            att_ref[order_ref[0]],
            own_ref[:, :, pl.ds(start, width)].reshape(2 * HEAD_DIM, width),
            NN,
            preferred_element_type=F32,
        )
        for n in range(count):
            piece = pieces[side * count + n][...].reshape(2 * HEAD_DIM, width)
            acc = acc + lax.dot_general(
                att_ref[order_ref[n + 1]], piece, NN, preferred_element_type=F32
            )
        out_ref[:, pl.ds(start, width)] = acc.astype(BF16)


def project(order, att, own, mine, other, width=512):
    groups, rows, depth = att.shape
    columns = own.shape[2]
    piece = pl.BlockSpec((2, HEAD_DIM, width), lambda i, o: (0, 0, i))
    return pl.pallas_call(
        project_kernel,
        grid_spec=pltpu.PrefetchScalarGridSpec(
            num_scalar_prefetch=1,
            grid=(columns // 2 // width,),
            in_specs=[
                pl.BlockSpec((groups, rows, depth), lambda i, o: (0, 0, 0)),
                pl.BlockSpec((2, HEAD_DIM, columns), lambda i, o: (0, 0, 0)),
            ]
            + [piece] * (len(mine) + len(other)),
            out_specs=pl.BlockSpec((rows, columns), lambda i, o: (0, 0)),
        ),
        out_shape=jax.ShapeDtypeStruct((rows, columns), BF16),
        compiler_params=pltpu.CompilerParams(vmem_limit_bytes=VMEM_LIMIT),
        cost_estimate=cost(2 * rows * columns * groups * depth, groups * depth * columns * 2),
        name="project",
    )(order, att, own, *mine, *other)


def head_pairs(dx, dy, count=8):
    def to(place):
        x, y = place // 2, place % 2
        return (x + dx) % (count // 2) * 2 + (y + dy) % 2

    return [(place, to(place)) for place in range(count)]


def gather_weight(out_weight, core):
    half = out_weight.shape[2] // 2
    own = lax.dynamic_slice_in_dim(out_weight, core * half, half, 2)
    send = lambda value, dx, dy: lax.ppermute(value, "head", head_pairs(dx, dy))
    pieces = []
    beside = send(own, 0, 1)
    for value, dy in ((own, 0), (beside, 1)):
        if dy:
            pieces.append(((0, 1), beside))
        pieces.append(((-1, dy), send(value, 1, 0)))
        pieces.append(((1, dy), send(value, -1, 0)))
        pieces.append(((2, dy), send(pieces[-1][1], -1, 0)))
    swap = [(c, c ^ 1) for c in range(lax.axis_size("ctx"))]
    other = [lax.ppermute(piece, "ctx", swap) for _, piece in pieces]
    return [place for place, _ in pieces], [piece for _, piece in pieces], other


def planned(near, operands):
    query_states, key_states, value_states, block_pattern, helper_distances, out_weight = operands
    shard = lax.axis_index("ctx")
    shards = lax.axis_size("ctx")
    place = lax.axis_index("head")
    core = shard % 2
    per_shard = query_states.shape[0] // BLOCK
    distances = (FAR, near)

    queries = split_queries(query_states)
    received = {}
    for h in range(2):
        for r in distances:
            received[h, r] = lax.ppermute(
                queries[h], "ctx", [(c, c - r) for c in range(r, shards)]
            )
    places, mine, other = gather_weight(out_weight, core)
    keys, values = split_kv(key_states, value_states)
    masks = {
        r: allowed_rows(block_pattern, jnp.minimum(shard + r, shards - 1), shard, per_shard)
        for r in (0,) + distances
    }
    own = local_attention(*queries, keys, values, masks[0])
    answers = {}
    for h in range(2):
        for r in distances:
            answer = helper_attention(h, received[h, r], keys, values, masks[r])
            answers[h, r] = lax.ppermute(
                answer, "ctx", [(c, c + r) for c in range(shards - r)]
            )
    valid = jnp.stack([(shard >= r).astype(jnp.int32) for r in distances])
    attended = merge(
        valid, own, *[[answers[h, r] for h in range(2)] for r in distances]
    )
    gathered = lax.all_to_all(attended, "head", 0, 0, tiled=False)
    x, y = place // 2, place % 2
    order = [place] + [(x + dx) % 4 * 2 + (y + dy) % 2 for dx, dy in places] + [core]
    return project(jnp.stack(order).astype(jnp.int32), gathered, out_weight, mine, other)


def per_device(*operands):
    helper_distances = operands[4]
    near = jnp.minimum(helper_distances[0], helper_distances[1])
    branches = [functools.partial(planned, r) for r in range(1, FAR)]
    return lax.switch(near - 1, branches, operands)


def solution(mesh):
    placed = (
        P("ctx", "head", None),
        P("ctx", "head", None),
        P("ctx", "head", None),
        P("head", None, None),
        P(),
        P("head", None, None),
    )
    return jax.shard_map(
        per_device, mesh=mesh, in_specs=placed, out_specs=P(("ctx", "head"), None), check_vma=False
    )
```

```python
import functools

import jax
import jax.numpy as jnp
from jax import lax
from jax.experimental import pallas as pl
from jax.experimental.pallas import tpu as pltpu
from jax.sharding import PartitionSpec as P

BLOCK = 128
HEAD_DIM = 128
NEG = -1e30
BIG = 1e30
SCALE = HEAD_DIM**-0.5 * 1.4426950408889634
FAR = 8
TILE = 256
PAIR = 2 * TILE
STAT_ROWS = 16
OUT_ROWS = HEAD_DIM + STAT_ROWS
BF16 = jnp.bfloat16
F32 = jnp.float32
NT = (((1,), (1,)), ((), ()))
NN = (((1,), (0,)), ((), ()))
MESH = pl.DeviceIdType.MESH
WHOLE = pl.BlockSpec(memory_space=pltpu.VMEM)
VMEM_LIMIT = 60 << 20


def three_parts(x):
    first = x.astype(BF16)
    rest = x - first.astype(F32)
    second = rest.astype(BF16)
    return [first.astype(F32), second.astype(F32), rest - second.astype(F32)]


def aligned(value, factor):
    return pl.multiple_of(value * factor, factor)


def whole_kernel(
    near, shards, places,
    pattern, q_raw, k_raw, v_raw, w_own, out_ref,
    wide, keys, values, queries, made, came, s_a, s_b, diag_a, diag_b, peak_ref,
    peak_start, acc_start, total_start, att_out, att_in, w_all,
    q_sent, q_came, made_sent, made_came, att_sent, att_came, w_sent, w_came,
):
    shard = lax.axis_index("ctx")
    place = lax.axis_index("head")
    core = lax.rem(shard, 2)
    x, y = place // 2, lax.rem(place, 2)
    xs = places // 2
    beside = 2 * x + 1 - y
    up = 2 * lax.rem(x + 1, xs) + y
    down = 2 * lax.rem(x + xs - 1, xs) + y
    twin = shard + 1 - 2 * core
    rows = keys.shape[1]
    blocks = rows // BLOCK
    chunks = rows // TILE
    tiles = rows // TILE
    slots = 6
    reach = (FAR, near)
    asked = [shard + r < shards for r in reach]
    helped = [shard >= r for r in reach]

    def to_ctx(index):
        return {"ctx": index}

    def to_head(index):
        return {"head": index}

    def remote(src, dst, sent, landed, device):
        return pltpu.make_async_remote_copy(
            src_ref=src, dst_ref=dst, send_sem=sent, recv_sem=landed,
            device_id=device, device_id_type=MESH,
        )

    barrier = pltpu.get_barrier_semaphore()
    pl.semaphore_signal(barrier, inc=1, device_id=to_ctx(twin), device_id_type=MESH)

    def greet(n, carry):
        other = lax.rem(place + n, places)
        pl.semaphore_signal(barrier, inc=1, device_id=to_head(other), device_id_type=MESH)
        return carry

    lax.fori_loop(1, places, greet, 0)
    for r, has, gets in zip(reach, asked, helped):
        @pl.when(has)
        def _():
            pl.semaphore_signal(barrier, inc=1, device_id=to_ctx(shard + r), device_id_type=MESH)

        @pl.when(gets)
        def _():
            pl.semaphore_signal(barrier, inc=1, device_id=to_ctx(shard - r), device_id_type=MESH)

    def split_queries(i, carry):
        wide[0] = q_raw[pl.ds(aligned(i, PAIR), PAIR), :].astype(F32)
        for h in range(2):
            queries[h, pl.ds(aligned(i, TILE), TILE), :] = wide[
                0, pl.ds(h, TILE, stride=2), :
            ].astype(BF16)
        return carry

    lax.fori_loop(0, tiles, split_queries, 0)
    peers = [jnp.where(flag, 1, 0) for flag in asked + helped]
    pl.semaphore_wait(barrier, places + peers[0] + peers[1] + peers[2] + peers[3])

    def query_copy(h, source):
        n = 2 * h + source
        return remote(
            queries.at[h], queries.at[2 + n], q_sent.at[n], q_came.at[n],
            to_ctx(jnp.where(helped[source], shard - reach[source], shard + reach[source])),
        )

    columns = w_own.shape[2] // 2
    mine = pl.ds(aligned(core, columns), columns)

    def weight_copy(n, device, slot, source=None, part=None):
        head = slice(None) if part is None else part
        src = (w_own if source is None else w_all.at[slot]).at[head, :, mine]
        return remote(src, w_all.at[slot, head, :, mine], w_sent.at[n], w_came.at[n], device)

    across = 2 * lax.rem(x + 2, xs) + y
    across_beside = 2 * lax.rem(x + 2, xs) + 1 - y
    up_beside = 2 * lax.rem(x + 1, xs) + 1 - y
    down_beside = 2 * lax.rem(x + xs - 1, xs) + 1 - y
    sends = {
        0: lambda: weight_copy(0, to_head(beside), place),
        1: lambda: weight_copy(1, to_head(up), place),
        2: lambda: weight_copy(2, to_head(down), place),
        3: lambda: weight_copy(3, to_head(up), down, True, 1),
        4: lambda: weight_copy(4, to_head(down), up, True, 0),
        5: lambda: weight_copy(5, to_head(up), beside, True),
        6: lambda: weight_copy(6, to_head(down), beside, True),
        7: lambda: weight_copy(7, to_head(beside), across, True),
    }
    origins = {
        0: (beside, None), 1: (down, None), 2: (up, None), 3: (across, 1), 4: (across, 0),
        5: (down_beside, None), 6: (up_beside, None), 7: (across_beside, None),
    }
    swaps = {8: beside, 9: down, 10: up, 11: across, 12: down_beside, 13: up_beside, 14: across_beside}

    def swap_copy(n):
        return weight_copy(n, to_ctx(twin), swaps[n], True)

    def weight_wait(n):
        slot, part = origins[n]
        weight_copy(n, to_head(beside), slot, True, part).wait_recv()

    for h in range(2):
        for source in range(2):
            @pl.when(helped[source])
            def _():
                query_copy(h, source).start()
        if h == 0:
            for n in range(3):
                sends[n]().start()

    def split_kv(i, carry):
        wide[0] = k_raw[pl.ds(aligned(i, PAIR), PAIR), :].astype(F32)
        wide[1] = v_raw[pl.ds(aligned(i, PAIR), PAIR), :].astype(F32)
        for h in range(2):
            to = pl.ds(aligned(i, TILE), TILE)
            keys[h, to, :] = wide[0, pl.ds(h, TILE, stride=2), :].astype(BF16)
            values[h, :, to] = wide[1, pl.ds(h, TILE, stride=2), :].T.astype(BF16)
        return carry

    lax.fori_loop(0, tiles, split_kv, 0)

    def where_of(t):
        slot, u = t // tiles, lax.rem(t, tiles)
        h = jnp.where(slot < 2, slot, (slot - 2) // 2)
        return slot, u, h

    def flags(slot, u, i):
        limit = jnp.where(slot < 2, 2 * u, blocks)
        parts = []
        for b in range(2):
            bit = pattern[(slot * blocks + 2 * u + b) * blocks + i]
            bit = jnp.where(i < limit + b, bit, 0)
            parts.append(jnp.full((8, BLOCK), bit, jnp.int32))
        return jnp.concatenate(parts, 1) > 0

    place_k = lax.broadcasted_iota(jnp.int32, (TILE, TILE), 0)
    place_q = lax.broadcasted_iota(jnp.int32, (TILE, TILE), 1)

    def phase(t1, t2, first, second, odd):
        s_first, diag_first = first
        s_second, diag_second = second
        slot2, u2, h2 = where_of(t2)
        peak2 = peak_ref[...]
        if t1 is not None:
            slot1, u1, h1 = where_of(t1)
            q = queries[slot1, pl.ds(aligned(u1, TILE), TILE), :]

            @pl.when(t2 < 2 * tiles)
            def _():
                here = pl.ds(aligned(u1, TILE), TILE)
                s = lax.dot_general(keys[h1, here, :], q, NT, preferred_element_type=F32)
                same = (place_k // BLOCK) == (place_q // BLOCK)
                s = jnp.where(same & (place_k <= place_q) & (slot1 < 2), s, NEG)
                diag_first[...] = s
                peak_start[...] = s.reshape(TILE // 8, 8, TILE).max(0)
                p = jnp.exp2((diag_second[...].reshape(TILE // 8, 8, TILE) - peak2) * SCALE)
                total_start[...] = p.sum(0)
                there = pl.ds(aligned(u2, TILE), TILE)
                acc_start[...] = lax.dot_general(
                    values[h2, :, there], p.reshape(TILE, TILE).astype(BF16), NN,
                    preferred_element_type=F32,
                )

            @pl.when(t2 == 2 * tiles)
            def _():
                peak_start[...] = jnp.full_like(peak_start, NEG)
                total_start[...] = jnp.zeros_like(total_start)
                acc_start[...] = jnp.zeros_like(acc_start)

            peak1 = peak_start[...]
        total = total_start[...]
        acc = acc_start[...]
        for j in range(chunks):
            chunk = slice(j * TILE, (j + 1) * TILE)
            if t1 is not None:
                s = lax.dot_general(keys[h1, chunk, :], q, NT, preferred_element_type=F32)
                s_first[chunk] = s
                for b in range(2):
                    block_peak = s[b * BLOCK : (b + 1) * BLOCK].reshape(BLOCK // 8, 8, TILE).max(0)
                    allowed = flags(slot1, u1, 2 * j + b)
                    peak1 = jnp.maximum(peak1, jnp.where(allowed, block_peak, NEG))
            parts = []
            for b in range(2):
                i = 2 * j + b
                shift = jnp.where(flags(slot2, u2, i), peak2, BIG)
                s2 = s_second[i * BLOCK : (i + 1) * BLOCK].reshape(BLOCK // 8, 8, TILE)
                p = jnp.exp2((s2 - shift) * SCALE)
                total = total + p.sum(0)
                parts.append(p.reshape(BLOCK, TILE).astype(BF16))
            acc = acc + lax.dot_general(
                values[h2, :, chunk], jnp.concatenate(parts, 0), NN, preferred_element_type=F32
            )
        total = total.sum(0, keepdims=True)
        inverse = jnp.where(total > 0, 1.0 / jnp.where(total > 0, total, 1.0), 0.0)
        stats = three_parts(peak2[0:1]) + three_parts(total)
        stats.append(jnp.zeros((STAT_ROWS - 6, TILE), F32))
        made[t2 // 2, :, odd * TILE : (odd + 1) * TILE] = jnp.concatenate(
            [acc * inverse] + stats, 0
        ).astype(BF16)
        if t1 is not None:
            peak_ref[...] = jnp.broadcast_to(peak1.max(0, keepdims=True), (8, TILE))

    pairs = tiles // 2
    own_pairs = 2 * pairs

    def answer_copy(pair, source):
        n = pair - own_pairs
        return remote(
            made.at[pair], came.at[n], made_sent.at[n], made_came.at[n],
            to_ctx(jnp.where(asked[source], shard + reach[source], shard - reach[source])),
        )

    def send_answer(pair):
        for source in range(2):
            @pl.when((pair >= own_pairs) & (lax.rem(pair // pairs, 2) == source) & asked[source])
            def _():
                answer_copy(pair, source).start()

    def merge_pair(h, n):
        answers = [2 * h * pairs + n, (2 * h + 1) * pairs + n]
        for source in range(2):
            @pl.when(helped[source])
            def _():
                answer_copy(own_pairs + answers[source], source).wait_recv()
        for half in range(2):
            lanes = slice(half * TILE, (half + 1) * TILE)
            pieces = []
            for r in range(3):
                part = (made[h * pairs + n, :, lanes] if r == 0 else came[answers[r - 1], :, lanes])
                part = part.astype(F32)
                if r > 0:
                    part = jnp.where(helped[r - 1], part, 0.0)
                stats = part[HEAD_DIM : HEAD_DIM + 8]
                peak = stats[0:1] + stats[1:2] + stats[2:3]
                total = stats[3:4] + stats[4:5] + stats[5:6]
                if r > 0:
                    peak = jnp.where(helped[r - 1], peak, NEG)
                pieces.append((part[:HEAD_DIM], peak, total))
            top = jnp.maximum(jnp.maximum(pieces[0][1], pieces[1][1]), pieces[2][1])
            factors = [jnp.exp2((peak - top) * SCALE) * total for _, peak, total in pieces]
            inverse = 1.0 / (factors[0] + factors[1] + factors[2])
            mixed = sum(part * (factor * inverse) for (part, _, _), factor in zip(pieces, factors))
            att_out[h, 2 * n + half] = mixed.T.astype(BF16)

    def att_copy(h, u):
        return remote(
            att_out.at[h, u], att_in.at[place, h], att_sent.at[h, u], att_came.at[h, place],
            to_head(u),
        )

    def send_rows(h, n):
        for half in range(2):
            u = 2 * n + half

            @pl.when(u == place)
            def _():
                att_in[place, h] = att_out[h, u]

            @pl.when(u != place)
            def _():
                att_copy(h, u).start()

    peak_ref[...] = jnp.zeros_like(peak_ref)
    diag_b[...] = jnp.full_like(diag_b, NEG)
    a, b = (s_a, diag_a), (s_b, diag_b)
    steps = slots * tiles // 2

    def step(i, carry):
        for n in range(4):
            @pl.when((i == own_pairs + n * pairs) & asked[n % 2])
            def _():
                query_copy(n // 2, n % 2).wait_recv()

        @pl.when(i == own_pairs + 4)
        def _():
            for n in (1, 2):
                weight_wait(n)
            for n in (3, 4):
                sends[n]().start()
            weight_wait(0)
            for n in (5, 6):
                sends[n]().start()
            for n in (8, 9, 10):
                swap_copy(n).start()

        @pl.when(i == own_pairs + 12)
        def _():
            for n in (3, 4):
                weight_wait(n)
            sends[7]().start()
            swap_copy(11).start()

        phase(2 * i, jnp.maximum(2 * i - 1, 0), a, b, 1)
        phase(2 * i + 1, 2 * i, b, a, 0)
        send_answer(i - 1)

        late = i - (steps - pairs)

        @pl.when(late >= 1)
        def _():
            send_rows(0, late - 1)

        @pl.when(late >= 0)
        def _():
            merge_pair(0, late)

        return carry

    lax.fori_loop(0, steps, step, 0)
    phase(None, slots * tiles - 1, a, b, 1)
    send_rows(0, pairs - 1)
    send_answer(steps - 1)

    def merge_rest(n, carry):
        @pl.when(n < pairs)
        def _():
            merge_pair(1, n)

        @pl.when(n >= 1)
        def _():
            send_rows(1, n - 1)

        return carry

    lax.fori_loop(0, pairs + 1, merge_rest, 0)
    for n in (5, 6):
        weight_wait(n)
    for n in (12, 13):
        swap_copy(n).start()
    weight_wait(7)
    swap_copy(14).start()
    for n in swaps:
        swap_wait = weight_copy(n, to_ctx(twin), swaps[n], True)
        other = pl.ds(aligned(1 - core, columns), columns)
        remote(
            w_all.at[swaps[n], :, :, other], w_all.at[swaps[n], :, :, other],
            w_sent.at[n], w_came.at[n], to_ctx(twin),
        ).wait_recv()
        swap_wait.wait_send()
    for n in range(8):
        sends[n]().wait_send()

    def rows_wait(n, carry):
        g = lax.rem(place + n, places)
        for h in range(2):
            remote(
                att_out.at[h, g], att_in.at[g, h], att_sent.at[h, g], att_came.at[h, g], to_head(g)
            ).wait()
        return carry

    lax.fori_loop(1, places, rows_wait, 0)

    width = 256

    def project(c, carry):
        cols = pl.ds(aligned(c, width), width)
        acc = None
        for n in range(places):
            g = lax.rem(place + n, places)
            left = jnp.concatenate([att_in[g, 0], att_in[g, 1]], 1)
            right = (w_own[:, :, cols] if n == 0 else w_all[g, :, :, cols]).reshape(
                2 * HEAD_DIM, width
            )
            term = lax.dot_general(left, right, NN, preferred_element_type=F32)
            acc = term if acc is None else acc + term
        out_ref[:, cols] = acc.astype(BF16)
        return carry

    lax.fori_loop(0, out_ref.shape[1] // width, project, 0)

    for source in range(2):
        @pl.when(helped[source])
        def _():
            for h in range(2):
                query_copy(h, source).wait_send()

        @pl.when(asked[source])
        def _():
            for h in range(2):
                for n in range(pairs):
                    answer_copy(own_pairs + (2 * h + source) * pairs + n, source).wait_send()


def planned(near, shards, places, pattern, q, k, v, w):
    rows = q.shape[0]
    flat = lambda array: array.reshape(rows * 2, HEAD_DIM)
    tiles = rows // TILE
    pairs = tiles // 2
    answers = 4 * pairs
    dma = pltpu.SemaphoreType.DMA
    vm = pltpu.VMEM
    return pl.pallas_call(
        functools.partial(whole_kernel, near, shards, places),
        in_specs=[pl.BlockSpec(memory_space=pltpu.SMEM)] + [WHOLE] * 4,
        out_specs=WHOLE,
        out_shape=jax.ShapeDtypeStruct((rows // places, w.shape[2]), BF16),
        scratch_shapes=[
            vm((2, PAIR, HEAD_DIM), F32),
            vm((2, rows, HEAD_DIM), BF16),
            vm((2, HEAD_DIM, rows), BF16),
            vm((6, rows, HEAD_DIM), BF16),
            vm((2 * pairs + answers, OUT_ROWS, PAIR), BF16),
            vm((answers, OUT_ROWS, PAIR), BF16),
            vm((rows, TILE), F32),
            vm((rows, TILE), F32),
            vm((TILE, TILE), F32),
            vm((TILE, TILE), F32),
            vm((8, TILE), F32),
            vm((8, TILE), F32),
            vm((HEAD_DIM, TILE), F32),
            vm((8, TILE), F32),
            vm((2, places, TILE, HEAD_DIM), BF16),
            vm((places, 2, TILE, HEAD_DIM), BF16),
            vm((places, 2, HEAD_DIM, w.shape[2]), BF16),
            dma((4,)), dma((4,)), dma((answers,)), dma((answers,)),
            dma((2, places)), dma((2, places)), dma((15,)), dma((15,)),
        ],
        compiler_params=pltpu.CompilerParams(
            collective_id=near, has_side_effects=True, vmem_limit_bytes=VMEM_LIMIT
        ),
        name=f"whole_{near}",
    )(pattern, flat(q), flat(k), flat(v), w)


def per_device(query_states, key_states, value_states, block_pattern, helper_distances, out_weight):
    shard = lax.axis_index("ctx")
    shards = lax.axis_size("ctx")
    places = lax.axis_size("head")
    near = jnp.minimum(helper_distances[0], helper_distances[1])
    blocks = query_states.shape[0] // BLOCK

    def bits(distance):
        asker = jnp.minimum(shard + distance, shards - 1)
        starts = (jnp.zeros((), jnp.int32), asker * blocks, shard * blocks)
        return lax.dynamic_slice(block_pattern, starts, (2, blocks, blocks))

    own, far, close = bits(0), bits(FAR), bits(near)
    pattern = jnp.concatenate([own, far[:1], close[:1], far[1:], close[1:]]).reshape(-1)
    branches = [functools.partial(planned, r, shards, places) for r in range(1, FAR)]
    return lax.switch(
        near - 1, branches, pattern, query_states, key_states, value_states, out_weight
    )


def solution(mesh):
    placed = (
        P("ctx", "head", None),
        P("ctx", "head", None),
        P("ctx", "head", None),
        P("head", None, None),
        P(),
        P("head", None, None),
    )
    return jax.shard_map(
        per_device, mesh=mesh, in_specs=placed, out_specs=P(("ctx", "head"), None), check_vma=False
    )
```

```python
import functools

import jax
import jax.numpy as jnp
from jax import lax
from jax.experimental import pallas as pl
from jax.experimental.pallas import tpu as pltpu
from jax.sharding import PartitionSpec as P

BLOCK = 128
HEAD_DIM = 128
NEG = -1e30
BIG = 1e30
SCALE = HEAD_DIM**-0.5 * 1.4426950408889634
FAR = 8
TILE = 256
PAIR = 2 * TILE
STAT_ROWS = 16
OUT_ROWS = HEAD_DIM + STAT_ROWS
BF16 = jnp.bfloat16
F32 = jnp.float32
NT = (((1,), (1,)), ((), ()))
NN = (((1,), (0,)), ((), ()))
MESH = pl.DeviceIdType.MESH
WHOLE = pl.BlockSpec(memory_space=pltpu.VMEM)
VMEM_LIMIT = 60 << 20
LAG = 3
EVENTS = (10, 13, 16, 23)


def three_parts(x):
    first = x.astype(BF16)
    rest = x - first.astype(F32)
    second = rest.astype(BF16)
    return [first.astype(F32), second.astype(F32), rest - second.astype(F32)]


def aligned(value, factor):
    return pl.multiple_of(value * factor, factor)


def whole_kernel(
    near, shards, places,
    pattern_all, q_raw, k_raw, v_raw, w_own, out_ref,
    pattern, wide, keys, values, queries, made, came, s_a, s_b, diag_a, diag_b, peak_ref,
    peak_start, acc_start, total_start, att_out, att_in, w_all,
    q_sent, q_came, made_sent, made_came, att_sent, att_came, w_sent, w_came, spread_sent, spread_came, bits_came,
):
    shard = lax.axis_index("ctx")
    place = lax.axis_index("head")
    core = lax.rem(shard, 2)
    x, y = place // 2, lax.rem(place, 2)
    xs = places // 2
    beside = 2 * x + 1 - y
    up = 2 * lax.rem(x + 1, xs) + y
    down = 2 * lax.rem(x + xs - 1, xs) + y
    twin = shard + 1 - 2 * core
    z = lax.rem(shard // 2, 4)
    odd_z = lax.rem(z, 2)
    z_up = shard + 2 * lax.rem(z + 1, 4) - 2 * z
    z_down = shard + 2 * lax.rem(z + 3, 4) - 2 * z
    rows = keys.shape[1]
    blocks = rows // BLOCK
    chunks = rows // TILE
    tiles = rows // TILE
    pairs = tiles // 2
    groups = 2 * pairs
    reach = (FAR, near)
    asked = [shard + r < shards for r in reach]
    helped = [shard >= r for r in reach]

    def to_ctx(index):
        return {"ctx": index}

    def to_head(index):
        return {"head": index}

    def remote(src, dst, sent, landed, device):
        return pltpu.make_async_remote_copy(
            src_ref=src, dst_ref=dst, send_sem=sent, recv_sem=landed,
            device_id=device, device_id_type=MESH,
        )

    def bits_copy(source):
        asker = shard if source == 0 else jnp.minimum(shard + reach[source - 1], shards - 1)
        return pltpu.make_async_copy(
            pattern_all.at[:, pl.ds(aligned(asker, blocks), blocks), :],
            pattern.at[source],
            bits_came.at[source],
        )

    for source in range(3):
        bits_copy(source).start()

    barrier = pltpu.get_barrier_semaphore()
    for other in (twin, z_up, z_down):
        pl.semaphore_signal(barrier, inc=1, device_id=to_ctx(other), device_id_type=MESH)

    def greet(n, carry):
        other = lax.rem(place + n, places)
        pl.semaphore_signal(barrier, inc=1, device_id=to_head(other), device_id_type=MESH)
        return carry

    lax.fori_loop(1, places, greet, 0)
    for r, has, gets in zip(reach, asked, helped):
        @pl.when(has)
        def _():
            pl.semaphore_signal(barrier, inc=1, device_id=to_ctx(shard + r), device_id_type=MESH)

        @pl.when(gets)
        def _():
            pl.semaphore_signal(barrier, inc=1, device_id=to_ctx(shard - r), device_id_type=MESH)

    def split_queries(i, carry):
        wide[0] = q_raw[pl.ds(aligned(i, PAIR), PAIR), :].astype(F32)
        for h in range(2):
            queries[h, pl.ds(aligned(i, TILE), TILE), :] = wide[
                0, pl.ds(h, TILE, stride=2), :
            ].astype(BF16)
        return carry

    lax.fori_loop(0, tiles, split_queries, 0)
    peers = [jnp.where(flag, 1, 0) for flag in asked + helped]
    pl.semaphore_wait(barrier, places + 2 + peers[0] + peers[1] + peers[2] + peers[3])

    def query_copy(n, source):
        h, rows_here = n // pairs, pl.ds(aligned(lax.rem(n, pairs), PAIR), PAIR)
        sem = source * groups + n
        return remote(
            queries.at[h, rows_here], queries.at[2 + 2 * h + source, rows_here],
            q_sent.at[sem], q_came.at[sem],
            to_ctx(jnp.where(helped[source], shard - reach[source], shard + reach[source])),
        )

    def send_queries(n, carry):
        for source in range(2):
            @pl.when(helped[source])
            def _():
                query_copy(n, source).start()

        return carry

    columns = w_own.shape[2] // 2
    share = columns * 3 // 16
    direct = pl.ds(aligned(core * 16 + odd_z * 6, columns // 16), columns * 5 // 8)
    lacking = pl.ds(aligned(core * 16 + (1 - odd_z) * 10, columns // 16), 2 * share)

    def block(parity, second):
        return pl.ds(aligned(core * 16 + parity * 10 + second * 3, columns // 16), share)

    def weight_copy(n, device, slot, cols, source=None, part=None, sent=None, came=None):
        head = slice(None) if part is None else part
        src = (w_own if source is None else w_all.at[slot]).at[head, :, cols]
        sent, came = (w_sent if sent is None else sent), (w_came if came is None else came)
        return remote(src, w_all.at[slot, head, :, cols], sent.at[n], came.at[n], device)

    def slot_of(p):
        p = jnp.asarray(p, jnp.int32)
        side = jnp.where((p == 0) | (p >= 4), 1 - y, y)
        kind = lax.rem(p, 3)
        hop = jnp.where(p == 0, 0, jnp.where(kind == 1, xs - 1, jnp.where(kind == 2, 1, 2)))
        return 2 * lax.rem(x + hop, xs) + side

    routes = [
        (beside, None, None), (up, None, None), (down, None, None),
        (up, 1, 1), (down, 2, 0), (up, 0, None), (down, 0, None), (up, 4, 1), (down, 5, 0),
    ]
    arrivals = [(0, None), (1, None), (2, None), (3, 1), (3, 0), (4, None), (5, None), (6, 1), (6, 0)]

    def forward(n):
        device, piece, part = routes[n]
        slot = place if piece is None else slot_of(piece)
        return weight_copy(n, to_head(device), slot, direct, piece, part)

    def arrived(n):
        piece, part = arrivals[n]
        weight_copy(n, to_head(beside), slot_of(piece), direct, True, part).wait_recv()

    def spread_copy(p, kind):
        device = (z_down, z_up, twin, twin)[kind]
        cols = (block(odd_z, 0), block(odd_z, 1), direct, lacking)[kind]
        return weight_copy(
            4 * p + kind, to_ctx(device), slot_of(p), cols, True, None, spread_sent, spread_came
        )

    def spread_wait(p, kind):
        theirs = (1 - core) * 16
        cols = (
            block(1 - odd_z, 0), block(1 - odd_z, 1),
            pl.ds(aligned(theirs + odd_z * 6, columns // 16), columns * 5 // 8),
            pl.ds(aligned(theirs + (1 - odd_z) * 10, columns // 16), 2 * share),
        )[kind]
        device = (z_up, z_down, twin, twin)[kind]
        weight_copy(
            4 * p + kind, to_ctx(device), slot_of(p), cols, True, None, spread_sent, spread_came
        ).wait_recv()

    def spread(first, last):
        def body(p, carry):
            for kind in range(3):
                spread_copy(p, kind).start()
            return carry

        lax.fori_loop(first, last + 1, body, 0)

    def settle(first, last):
        def body(p, carry):
            for kind in range(2):
                spread_wait(p, kind)
            spread_copy(p, 3).start()
            return carry

        lax.fori_loop(first, last + 1, body, 0)

    lax.fori_loop(0, pairs, send_queries, 0)
    for n in range(3):
        forward(n).start()
    lax.fori_loop(pairs, groups, send_queries, 0)

    def split_kv(i, carry):
        wide[0] = k_raw[pl.ds(aligned(i, PAIR), PAIR), :].astype(F32)
        wide[1] = v_raw[pl.ds(aligned(i, PAIR), PAIR), :].astype(F32)
        for h in range(2):
            to = pl.ds(aligned(i, TILE), TILE)
            keys[h, to, :] = wide[0, pl.ds(h, TILE, stride=2), :].astype(BF16)
            values[h, :, to] = wide[1, pl.ds(h, TILE, stride=2), :].T.astype(BF16)
        return carry

    lax.fori_loop(0, tiles, split_kv, 0)

    def where_of(t):
        pair = t // 2
        kind, n = lax.rem(pair, 3), pair // 3
        h = n // pairs
        u = 2 * lax.rem(n, pairs) + lax.rem(t, 2)
        slot = jnp.where(kind == 0, h, 1 + 2 * h + kind)
        return kind, slot, u, h, kind * groups + n

    def flags(kind, h, u, i):
        limit = jnp.where(kind == 0, 2 * u, blocks)
        parts = []
        for b in range(2):
            bit = pattern[kind, h, 2 * u + b, shard * blocks + i]
            bit = jnp.where(i < limit + b, bit, 0)
            parts.append(jnp.full((8, BLOCK), bit, jnp.int32))
        return jnp.concatenate(parts, 1) > 0

    place_k = lax.broadcasted_iota(jnp.int32, (TILE, TILE), 0)
    place_q = lax.broadcasted_iota(jnp.int32, (TILE, TILE), 1)

    def phase(t1, t2, first, second, odd):
        s_first, diag_first = first
        s_second, diag_second = second
        kind2, slot2, u2, h2, made2 = where_of(t2)
        peak2 = peak_ref[...]
        if t1 is not None:
            kind1, slot1, u1, h1, made1 = where_of(t1)
            q = queries[slot1, pl.ds(aligned(u1, TILE), TILE), :]

            @pl.when((kind1 == 0) | (kind2 == 0))
            def _():
                here = pl.ds(aligned(u1, TILE), TILE)
                s = lax.dot_general(keys[h1, here, :], q, NT, preferred_element_type=F32)
                same = (place_k // BLOCK) == (place_q // BLOCK)
                s = jnp.where(same & (place_k <= place_q) & (kind1 == 0), s, NEG)
                diag_first[...] = s
                peak_start[...] = s.reshape(TILE // 8, 8, TILE).max(0)
                shift = jnp.where(kind2 == 0, peak2, BIG)
                p = jnp.exp2((diag_second[...].reshape(TILE // 8, 8, TILE) - shift) * SCALE)
                total_start[...] = p.sum(0)
                there = pl.ds(aligned(u2, TILE), TILE)
                acc_start[...] = lax.dot_general(
                    values[h2, :, there], p.reshape(TILE, TILE).astype(BF16), NN,
                    preferred_element_type=F32,
                )

            @pl.when((kind1 != 0) & (kind2 != 0))
            def _():
                peak_start[...] = jnp.full_like(peak_start, NEG)
                total_start[...] = jnp.zeros_like(total_start)
                acc_start[...] = jnp.zeros_like(acc_start)

            peak1 = peak_start[...]
        total = total_start[...]
        acc = acc_start[...]
        for j in range(chunks):
            chunk = slice(j * TILE, (j + 1) * TILE)
            if t1 is not None:
                s = lax.dot_general(keys[h1, chunk, :], q, NT, preferred_element_type=F32)
                s_first[chunk] = s
                for b in range(2):
                    block_peak = s[b * BLOCK : (b + 1) * BLOCK].reshape(BLOCK // 8, 8, TILE).max(0)
                    allowed = flags(kind1, h1, u1, 2 * j + b)
                    peak1 = jnp.maximum(peak1, jnp.where(allowed, block_peak, NEG))
            parts = []
            for b in range(2):
                i = 2 * j + b
                shift = jnp.where(flags(kind2, h2, u2, i), peak2, BIG)
                s2 = s_second[i * BLOCK : (i + 1) * BLOCK].reshape(BLOCK // 8, 8, TILE)
                p = jnp.exp2((s2 - shift) * SCALE)
                total = total + p.sum(0)
                parts.append(p.reshape(BLOCK, TILE).astype(BF16))
            acc = acc + lax.dot_general(
                values[h2, :, chunk], jnp.concatenate(parts, 0), NN, preferred_element_type=F32
            )
        total = total.sum(0, keepdims=True)
        inverse = jnp.where(total > 0, 1.0 / jnp.where(total > 0, total, 1.0), 0.0)
        stats = three_parts(peak2[0:1]) + three_parts(total)
        stats.append(jnp.zeros((STAT_ROWS - 6, TILE), F32))
        made[made2, :, odd * TILE : (odd + 1) * TILE] = jnp.concatenate(
            [acc * inverse] + stats, 0
        ).astype(BF16)
        if t1 is not None:
            peak_ref[...] = jnp.broadcast_to(peak1.max(0, keepdims=True), (8, TILE))

    def answer_copy(n, source):
        sem = source * groups + n
        return remote(
            made.at[(1 + source) * groups + n], came.at[sem], made_sent.at[sem], made_came.at[sem],
            to_ctx(jnp.where(asked[source], shard + reach[source], shard - reach[source])),
        )

    def send_answer(i):
        for source in range(2):
            @pl.when((i >= 0) & (lax.rem(i + 3, 3) == 1 + source) & asked[source])
            def _():
                answer_copy(i // 3, source).start()

    def merge_pair(n):
        h = n // pairs
        for source in range(2):
            @pl.when(helped[source])
            def _():
                answer_copy(n, source).wait_recv()
        for half in range(2):
            lanes = slice(half * TILE, (half + 1) * TILE)
            pieces = []
            for r in range(3):
                part = made[n, :, lanes] if r == 0 else came[(r - 1) * groups + n, :, lanes]
                part = part.astype(F32)
                if r > 0:
                    part = jnp.where(helped[r - 1], part, 0.0)
                stats = part[HEAD_DIM : HEAD_DIM + 8]
                peak = stats[0:1] + stats[1:2] + stats[2:3]
                total = stats[3:4] + stats[4:5] + stats[5:6]
                if r > 0:
                    peak = jnp.where(helped[r - 1], peak, NEG)
                pieces.append((part[:HEAD_DIM], peak, total))
            top = jnp.maximum(jnp.maximum(pieces[0][1], pieces[1][1]), pieces[2][1])
            factors = [jnp.exp2((peak - top) * SCALE) * total for _, peak, total in pieces]
            inverse = 1.0 / (factors[0] + factors[1] + factors[2])
            mixed = sum(part * (factor * inverse) for (part, _, _), factor in zip(pieces, factors))
            att_out[h, 2 * lax.rem(n, pairs) + half] = mixed.T.astype(BF16)

    def att_copy(h, u):
        return remote(
            att_out.at[h, u], att_in.at[place, h], att_sent.at[h, u], att_came.at[h, place],
            to_head(u),
        )

    def send_rows(n):
        h = n // pairs
        for half in range(2):
            u = 2 * lax.rem(n, pairs) + half

            @pl.when(u == place)
            def _():
                att_in[place, h] = att_out[h, u]

            @pl.when(u != place)
            def _():
                att_copy(h, u).start()

    def combine(n):
        @pl.when((n >= 1) & (n <= groups))
        def _():
            send_rows(n - 1)

        @pl.when((n >= 0) & (n < groups))
        def _():
            merge_pair(n)

    peak_ref[...] = jnp.zeros_like(peak_ref)
    diag_a[...] = jnp.full_like(diag_a, NEG)
    diag_b[...] = jnp.full_like(diag_b, NEG)
    a, b = (s_a, diag_a), (s_b, diag_b)
    steps = 3 * groups
    lag = LAG
    for source in range(3):
        bits_copy(source).wait()

    def step(i, carry):
        for source in range(2):
            @pl.when((lax.rem(i, 3) == 1 + source) & asked[source])
            def _():
                query_copy(i // 3, source).wait_recv()

        @pl.when(i == EVENTS[0])
        def _():
            for n in (1, 2):
                arrived(n)
            for n in (3, 4):
                forward(n).start()
            spread(1, 2)

        @pl.when(i == EVENTS[1])
        def _():
            arrived(0)
            for n in (5, 6):
                forward(n).start()
            spread(0, 0)

        @pl.when(i == EVENTS[2])
        def _():
            for n in (3, 4):
                arrived(n)
            spread(3, 3)
            settle(1, 2)

        @pl.when(i == EVENTS[3])
        def _():
            for n in (5, 6):
                arrived(n)
            for n in (7, 8):
                forward(n).start()
            spread(4, 5)
            settle(0, 0)

        phase(2 * i, jnp.maximum(2 * i - 1, 0), a, b, 1)
        phase(2 * i + 1, 2 * i, b, a, 0)
        send_answer(i - 1)

        @pl.when(lax.rem(i, 3) == 0)
        def _():
            combine(i // 3 - lag)

        return carry

    lax.fori_loop(0, steps, step, 0)
    phase(None, 2 * steps - 1, a, b, 1)
    send_answer(steps - 1)

    def merge_rest(n, carry):
        combine(n)
        return carry

    lax.fori_loop(groups - lag, groups + 1, merge_rest, 0)
    for n in (7, 8):
        arrived(n)
    spread(6, 6)
    settle(3, 6)
    for n in range(9):
        forward(n).wait_send()

    def spread_end(p, carry):
        for kind in (2, 3):
            spread_wait(p, kind)
        for kind in range(4):
            spread_copy(p, kind).wait_send()
        return carry

    lax.fori_loop(0, 7, spread_end, 0)

    def rows_wait(n, carry):
        g = lax.rem(place + n, places)
        for h in range(2):
            remote(
                att_out.at[h, g], att_in.at[g, h], att_sent.at[h, g], att_came.at[h, g], to_head(g)
            ).wait()
        return carry

    lax.fori_loop(1, places, rows_wait, 0)

    width = 256

    def project(c, carry):
        cols = pl.ds(aligned(c, width), width)
        acc = None
        for n in range(places):
            g = lax.rem(place + n, places)
            left = jnp.concatenate([att_in[g, 0], att_in[g, 1]], 1)
            right = (w_own[:, :, cols] if n == 0 else w_all[g, :, :, cols]).reshape(
                2 * HEAD_DIM, width
            )
            term = lax.dot_general(left, right, NN, preferred_element_type=F32)
            acc = term if acc is None else acc + term
        out_ref[:, cols] = acc.astype(BF16)
        return carry

    lax.fori_loop(0, out_ref.shape[1] // width, project, 0)

    def sent_wait(n, carry):
        for source in range(2):
            @pl.when(helped[source])
            def _():
                query_copy(n, source).wait_send()

            @pl.when(asked[source])
            def _():
                answer_copy(n, source).wait_send()

        return carry

    lax.fori_loop(0, groups, sent_wait, 0)


def planned(near, shards, places, pattern, q, k, v, w):
    rows = q.shape[0]
    flat = lambda array: array.reshape(rows * 2, HEAD_DIM)
    tiles = rows // TILE
    pairs = tiles // 2
    answers = 4 * pairs
    dma = pltpu.SemaphoreType.DMA
    vm = pltpu.VMEM
    return pl.pallas_call(
        functools.partial(whole_kernel, near, shards, places),
        in_specs=[pl.BlockSpec(memory_space=pl.ANY)] + [WHOLE] * 4,
        out_specs=WHOLE,
        out_shape=jax.ShapeDtypeStruct((rows // places, w.shape[2]), BF16),
        scratch_shapes=[
            pltpu.SMEM((3, 2, rows // BLOCK, pattern.shape[2]), jnp.int32),
            vm((2, PAIR, HEAD_DIM), F32),
            vm((2, rows, HEAD_DIM), BF16),
            vm((2, HEAD_DIM, rows), BF16),
            vm((6, rows, HEAD_DIM), BF16),
            vm((2 * pairs + answers, OUT_ROWS, PAIR), BF16),
            vm((answers, OUT_ROWS, PAIR), BF16),
            vm((rows, TILE), F32),
            vm((rows, TILE), F32),
            vm((TILE, TILE), F32),
            vm((TILE, TILE), F32),
            vm((8, TILE), F32),
            vm((8, TILE), F32),
            vm((HEAD_DIM, TILE), F32),
            vm((8, TILE), F32),
            vm((2, places, TILE, HEAD_DIM), BF16),
            vm((places, 2, TILE, HEAD_DIM), BF16),
            vm((places, 2, HEAD_DIM, w.shape[2]), BF16),
            dma((answers,)), dma((answers,)), dma((answers,)), dma((answers,)),
            dma((2, places)), dma((2, places)), dma((9,)), dma((9,)), dma((28,)), dma((28,)), dma((3,)),
        ],
        compiler_params=pltpu.CompilerParams(
            collective_id=near, has_side_effects=True, vmem_limit_bytes=VMEM_LIMIT
        ),
        name=f"whole_{near}",
    )(pattern, flat(q), flat(k), flat(v), w)


def per_device(query_states, key_states, value_states, block_pattern, helper_distances, out_weight):
    shards, places = lax.axis_size("ctx"), lax.axis_size("head")
    near = jnp.minimum(helper_distances[0], helper_distances[1])
    branches = [functools.partial(planned, r, shards, places) for r in range(1, FAR)]
    return lax.switch(
        near - 1, branches, block_pattern, query_states, key_states, value_states, out_weight
    )


def solution(mesh):
    placed = (
        P("ctx", "head", None),
        P("ctx", "head", None),
        P("ctx", "head", None),
        P("head", None, None),
        P(),
        P("head", None, None),
    )
    return jax.shard_map(
        per_device, mesh=mesh, in_specs=placed, out_specs=P(("ctx", "head"), None), check_vma=False
    )
```

```python
import functools

import jax
import jax.numpy as jnp
from jax import lax
from jax.experimental import pallas as pl
from jax.experimental.pallas import tpu as pltpu
from jax.sharding import PartitionSpec as P

BLOCK = 128
HEAD_DIM = 128
NEG = -1e30
BIG = 1e30
SCALE = HEAD_DIM**-0.5 * 1.4426950408889634
FAR = 8
TILE = 256
PAIR = 2 * TILE
STAT_ROWS = 16
OUT_ROWS = HEAD_DIM + STAT_ROWS
BF16 = jnp.bfloat16
F32 = jnp.float32
NT = (((1,), (1,)), ((), ()))
NN = (((1,), (0,)), ((), ()))
MESH = pl.DeviceIdType.MESH
WHOLE = pl.BlockSpec(memory_space=pltpu.VMEM)
VMEM_LIMIT = 60 << 20
LAG = 3
EVENTS = (8, 10, 13, 18)


def three_parts(x):
    first = x.astype(BF16)
    rest = x - first.astype(F32)
    second = rest.astype(BF16)
    return [first.astype(F32), second.astype(F32), rest - second.astype(F32)]


def aligned(value, factor):
    return pl.multiple_of(value * factor, factor)


def whole_kernel(
    near, shards, places,
    pattern_all, q_raw, k_hbm, v_hbm, w_hbm, out_ref,
    pattern, k_raw, v_raw, w_own, loaded, wide, keys, values, queries, made, came, s_a, s_b, diag_a, diag_b, peak_ref,
    peak_start, acc_start, total_start, att_out, att_in, w_all,
    q_sent, q_came, made_sent, made_came, att_sent, att_came, w_sent, w_came, spread_sent, spread_came, bits_came,
):
    shard = lax.axis_index("ctx")
    place = lax.axis_index("head")
    core = lax.rem(shard, 2)
    x, y = place // 2, lax.rem(place, 2)
    xs = places // 2
    beside = 2 * x + 1 - y
    up = 2 * lax.rem(x + 1, xs) + y
    down = 2 * lax.rem(x + xs - 1, xs) + y
    twin = shard + 1 - 2 * core
    z = lax.rem(shard // 2, 4)
    odd_z = lax.rem(z, 2)
    z_up = shard + 2 * lax.rem(z + 1, 4) - 2 * z
    z_down = shard + 2 * lax.rem(z + 3, 4) - 2 * z
    rows = keys.shape[1]
    blocks = rows // BLOCK
    chunks = rows // TILE
    tiles = rows // TILE
    pairs = tiles // 2
    groups = 2 * pairs
    reach = (FAR, near)
    asked = [shard + r < shards for r in reach]
    helped = [shard >= r for r in reach]

    def to_ctx(index):
        return {"ctx": index}

    def to_head(index):
        return {"head": index}

    def remote(src, dst, sent, landed, device):
        return pltpu.make_async_remote_copy(
            src_ref=src, dst_ref=dst, send_sem=sent, recv_sem=landed,
            device_id=device, device_id_type=MESH,
        )

    def bits_copy(source):
        asker = shard if source == 0 else jnp.minimum(shard + reach[source - 1], shards - 1)
        return pltpu.make_async_copy(
            pattern_all.at[:, pl.ds(aligned(asker, blocks), blocks), :],
            pattern.at[source],
            bits_came.at[source],
        )

    loads = [
        pltpu.make_async_copy(src, dst, loaded.at[n])
        for n, (src, dst) in enumerate(((w_hbm, w_own), (k_hbm, k_raw), (v_hbm, v_raw)))
    ]
    for load in loads:
        load.start()
    for source in range(3):
        bits_copy(source).start()

    barrier = pltpu.get_barrier_semaphore()
    for other in (twin, z_up, z_down):
        pl.semaphore_signal(barrier, inc=1, device_id=to_ctx(other), device_id_type=MESH)

    def greet(n, carry):
        other = lax.rem(place + n, places)
        pl.semaphore_signal(barrier, inc=1, device_id=to_head(other), device_id_type=MESH)
        return carry

    lax.fori_loop(1, places, greet, 0)
    for r, has, gets in zip(reach, asked, helped):
        @pl.when(has)
        def _():
            pl.semaphore_signal(barrier, inc=1, device_id=to_ctx(shard + r), device_id_type=MESH)

        @pl.when(gets)
        def _():
            pl.semaphore_signal(barrier, inc=1, device_id=to_ctx(shard - r), device_id_type=MESH)

    def split_queries(i, carry):
        wide[0] = q_raw[pl.ds(aligned(i, PAIR), PAIR), :].astype(F32)
        for h in range(2):
            queries[h, pl.ds(aligned(i, TILE), TILE), :] = wide[
                0, pl.ds(h, TILE, stride=2), :
            ].astype(BF16)
        return carry

    lax.fori_loop(0, tiles, split_queries, 0)
    peers = [jnp.where(flag, 1, 0) for flag in asked + helped]
    pl.semaphore_wait(barrier, places + 2 + peers[0] + peers[1] + peers[2] + peers[3])

    def query_copy(n, source):
        h, rows_here = n // pairs, pl.ds(aligned(lax.rem(n, pairs), PAIR), PAIR)
        sem = source * groups + n
        return remote(
            queries.at[h, rows_here], queries.at[2 + 2 * h + source, rows_here],
            q_sent.at[sem], q_came.at[sem],
            to_ctx(jnp.where(helped[source], shard - reach[source], shard + reach[source])),
        )

    def send_queries(n, carry):
        for source in range(2):
            @pl.when(helped[source])
            def _():
                query_copy(n, source).start()

        return carry

    columns = w_own.shape[2] // 2
    share = columns * 3 // 16
    direct = pl.ds(aligned(core * 16 + odd_z * 6, columns // 16), columns * 5 // 8)
    lacking = pl.ds(aligned(core * 16 + (1 - odd_z) * 10, columns // 16), 2 * share)

    def block(parity, second):
        return pl.ds(aligned(core * 16 + parity * 10 + second * 3, columns // 16), share)

    def weight_copy(n, device, slot, cols, source=None, part=None, sent=None, came=None):
        head = slice(None) if part is None else part
        src = (w_own if source is None else w_all.at[slot]).at[head, :, cols]
        sent, came = (w_sent if sent is None else sent), (w_came if came is None else came)
        return remote(src, w_all.at[slot, head, :, cols], sent.at[n], came.at[n], device)

    def slot_of(p):
        p = jnp.asarray(p, jnp.int32)
        side = jnp.where((p == 0) | (p >= 4), 1 - y, y)
        kind = lax.rem(p, 3)
        hop = jnp.where(p == 0, 0, jnp.where(kind == 1, xs - 1, jnp.where(kind == 2, 1, 2)))
        return 2 * lax.rem(x + hop, xs) + side

    routes = [
        (beside, None, None), (up, None, None), (down, None, None),
        (up, 1, 1), (down, 2, 0), (up, 0, None), (down, 0, None), (up, 4, 1), (down, 5, 0),
    ]
    arrivals = [(0, None), (1, None), (2, None), (3, 1), (3, 0), (4, None), (5, None), (6, 1), (6, 0)]

    def forward(n):
        device, piece, part = routes[n]
        slot = place if piece is None else slot_of(piece)
        return weight_copy(n, to_head(device), slot, direct, piece, part)

    def arrived(n):
        piece, part = arrivals[n]
        weight_copy(n, to_head(beside), slot_of(piece), direct, True, part).wait_recv()

    def spread_copy(p, kind):
        device = (z_down, z_up, twin, twin)[kind]
        cols = (block(odd_z, 0), block(odd_z, 1), direct, lacking)[kind]
        return weight_copy(
            4 * p + kind, to_ctx(device), slot_of(p), cols, True, None, spread_sent, spread_came
        )

    def spread_wait(p, kind):
        theirs = (1 - core) * 16
        cols = (
            block(1 - odd_z, 0), block(1 - odd_z, 1),
            pl.ds(aligned(theirs + odd_z * 6, columns // 16), columns * 5 // 8),
            pl.ds(aligned(theirs + (1 - odd_z) * 10, columns // 16), 2 * share),
        )[kind]
        device = (z_up, z_down, twin, twin)[kind]
        weight_copy(
            4 * p + kind, to_ctx(device), slot_of(p), cols, True, None, spread_sent, spread_came
        ).wait_recv()

    def spread(first, last):
        def body(p, carry):
            for kind in range(3):
                spread_copy(p, kind).start()
            return carry

        lax.fori_loop(first, last + 1, body, 0)

    def settle(first, last):
        def body(p, carry):
            for kind in range(2):
                spread_wait(p, kind)
            spread_copy(p, 3).start()
            return carry

        lax.fori_loop(first, last + 1, body, 0)

    lax.fori_loop(0, pairs, send_queries, 0)
    loads[0].wait()
    for n in range(3):
        forward(n).start()
    lax.fori_loop(pairs, groups, send_queries, 0)

    def split_kv(i, carry):
        wide[0] = k_raw[pl.ds(aligned(i, PAIR), PAIR), :].astype(F32)
        wide[1] = v_raw[pl.ds(aligned(i, PAIR), PAIR), :].astype(F32)
        for h in range(2):
            to = pl.ds(aligned(i, TILE), TILE)
            keys[h, to, :] = wide[0, pl.ds(h, TILE, stride=2), :].astype(BF16)
            values[h, :, to] = wide[1, pl.ds(h, TILE, stride=2), :].T.astype(BF16)
        return carry

    for load in loads[1:]:
        load.wait()
    lax.fori_loop(0, tiles, split_kv, 0)

    def where_of(t):
        pair = t // 2
        kind, n = lax.rem(pair, 3), pair // 3
        h = n // pairs
        u = 2 * lax.rem(n, pairs) + lax.rem(t, 2)
        slot = jnp.where(kind == 0, h, 1 + 2 * h + kind)
        return kind, slot, u, h, kind * groups + n

    def flags(kind, h, u, i):
        limit = jnp.where(kind == 0, 2 * u, blocks)
        parts = []
        for b in range(2):
            bit = pattern[kind, h, 2 * u + b, shard * blocks + i]
            bit = jnp.where(i < limit + b, bit, 0)
            parts.append(jnp.full((8, BLOCK), bit, jnp.int32))
        return jnp.concatenate(parts, 1) > 0

    place_k = lax.broadcasted_iota(jnp.int32, (TILE, TILE), 0)
    place_q = lax.broadcasted_iota(jnp.int32, (TILE, TILE), 1)

    def phase(t1, t2, first, second, odd):
        s_first, diag_first = first
        s_second, diag_second = second
        kind2, slot2, u2, h2, made2 = where_of(t2)
        peak2 = peak_ref[...]
        if t1 is not None:
            kind1, slot1, u1, h1, made1 = where_of(t1)
            q = queries[slot1, pl.ds(aligned(u1, TILE), TILE), :]

            @pl.when((kind1 == 0) | (kind2 == 0))
            def _():
                here = pl.ds(aligned(u1, TILE), TILE)
                s = lax.dot_general(keys[h1, here, :], q, NT, preferred_element_type=F32)
                same = (place_k // BLOCK) == (place_q // BLOCK)
                s = jnp.where(same & (place_k <= place_q) & (kind1 == 0), s, NEG)
                diag_first[...] = s
                peak_start[...] = s.reshape(TILE // 8, 8, TILE).max(0)
                shift = jnp.where(kind2 == 0, peak2, BIG)
                p = jnp.exp2((diag_second[...].reshape(TILE // 8, 8, TILE) - shift) * SCALE)
                total_start[...] = p.sum(0)
                there = pl.ds(aligned(u2, TILE), TILE)
                acc_start[...] = lax.dot_general(
                    values[h2, :, there], p.reshape(TILE, TILE).astype(BF16), NN,
                    preferred_element_type=F32,
                )

            @pl.when((kind1 != 0) & (kind2 != 0))
            def _():
                peak_start[...] = jnp.full_like(peak_start, NEG)
                total_start[...] = jnp.zeros_like(total_start)
                acc_start[...] = jnp.zeros_like(acc_start)

            peak1 = peak_start[...]
        total = total_start[...]
        acc = acc_start[...]
        for j in range(chunks):
            chunk = slice(j * TILE, (j + 1) * TILE)
            if t1 is not None:
                s = lax.dot_general(keys[h1, chunk, :], q, NT, preferred_element_type=F32)
                s_first[chunk] = s
                for b in range(2):
                    block_peak = s[b * BLOCK : (b + 1) * BLOCK].reshape(BLOCK // 8, 8, TILE).max(0)
                    allowed = flags(kind1, h1, u1, 2 * j + b)
                    peak1 = jnp.maximum(peak1, jnp.where(allowed, block_peak, NEG))
            parts = []
            for b in range(2):
                i = 2 * j + b
                shift = jnp.where(flags(kind2, h2, u2, i), peak2, BIG)
                s2 = s_second[i * BLOCK : (i + 1) * BLOCK].reshape(BLOCK // 8, 8, TILE)
                p = jnp.exp2((s2 - shift) * SCALE)
                total = total + p.sum(0)
                parts.append(p.reshape(BLOCK, TILE).astype(BF16))
            acc = acc + lax.dot_general(
                values[h2, :, chunk], jnp.concatenate(parts, 0), NN, preferred_element_type=F32
            )
        total = total.sum(0, keepdims=True)
        inverse = jnp.where(total > 0, 1.0 / jnp.where(total > 0, total, 1.0), 0.0)
        stats = three_parts(peak2[0:1]) + three_parts(total)
        stats.append(jnp.zeros((STAT_ROWS - 6, TILE), F32))
        made[made2, :, odd * TILE : (odd + 1) * TILE] = jnp.concatenate(
            [acc * inverse] + stats, 0
        ).astype(BF16)
        if t1 is not None:
            peak_ref[...] = jnp.broadcast_to(peak1.max(0, keepdims=True), (8, TILE))

    def answer_copy(n, source):
        sem = source * groups + n
        return remote(
            made.at[(1 + source) * groups + n], came.at[sem], made_sent.at[sem], made_came.at[sem],
            to_ctx(jnp.where(asked[source], shard + reach[source], shard - reach[source])),
        )

    def send_answer(i):
        for source in range(2):
            @pl.when((i >= 0) & (lax.rem(i + 3, 3) == 1 + source) & asked[source])
            def _():
                answer_copy(i // 3, source).start()

    def merge_pair(n):
        h = n // pairs
        for source in range(2):
            @pl.when(helped[source])
            def _():
                answer_copy(n, source).wait_recv()
        for half in range(2):
            lanes = slice(half * TILE, (half + 1) * TILE)
            pieces = []
            for r in range(3):
                part = made[n, :, lanes] if r == 0 else came[(r - 1) * groups + n, :, lanes]
                part = part.astype(F32)
                if r > 0:
                    part = jnp.where(helped[r - 1], part, 0.0)
                stats = part[HEAD_DIM : HEAD_DIM + 8]
                peak = stats[0:1] + stats[1:2] + stats[2:3]
                total = stats[3:4] + stats[4:5] + stats[5:6]
                if r > 0:
                    peak = jnp.where(helped[r - 1], peak, NEG)
                pieces.append((part[:HEAD_DIM], peak, total))
            top = jnp.maximum(jnp.maximum(pieces[0][1], pieces[1][1]), pieces[2][1])
            factors = [jnp.exp2((peak - top) * SCALE) * total for _, peak, total in pieces]
            inverse = 1.0 / (factors[0] + factors[1] + factors[2])
            mixed = sum(part * (factor * inverse) for (part, _, _), factor in zip(pieces, factors))
            att_out[h, 2 * lax.rem(n, pairs) + half] = mixed.T.astype(BF16)

    def att_copy(h, u):
        return remote(
            att_out.at[h, u], att_in.at[place, h], att_sent.at[h, u], att_came.at[h, place],
            to_head(u),
        )

    def send_rows(n):
        h = n // pairs
        for half in range(2):
            u = 2 * lax.rem(n, pairs) + half

            @pl.when(u == place)
            def _():
                att_in[place, h] = att_out[h, u]

            @pl.when(u != place)
            def _():
                att_copy(h, u).start()

    def combine(n):
        @pl.when((n >= 1) & (n <= groups))
        def _():
            send_rows(n - 1)

        @pl.when((n >= 0) & (n < groups))
        def _():
            merge_pair(n)

    peak_ref[...] = jnp.zeros_like(peak_ref)
    diag_a[...] = jnp.full_like(diag_a, NEG)
    diag_b[...] = jnp.full_like(diag_b, NEG)
    a, b = (s_a, diag_a), (s_b, diag_b)
    steps = 3 * groups
    lag = LAG
    for source in range(3):
        bits_copy(source).wait()

    def step(i, carry):
        for source in range(2):
            @pl.when((lax.rem(i, 3) == 1 + source) & asked[source])
            def _():
                query_copy(i // 3, source).wait_recv()

        @pl.when(i == EVENTS[0])
        def _():
            for n in (1, 2):
                arrived(n)
            for n in (3, 4):
                forward(n).start()
            spread(1, 2)

        @pl.when(i == EVENTS[1])
        def _():
            arrived(0)
            for n in (5, 6):
                forward(n).start()
            spread(0, 0)

        @pl.when(i == EVENTS[2])
        def _():
            for n in (3, 4):
                arrived(n)
            spread(3, 3)
            settle(1, 2)

        @pl.when(i == EVENTS[3])
        def _():
            for n in (5, 6):
                arrived(n)
            for n in (7, 8):
                forward(n).start()
            spread(4, 5)
            settle(0, 0)

        phase(2 * i, jnp.maximum(2 * i - 1, 0), a, b, 1)
        phase(2 * i + 1, 2 * i, b, a, 0)
        send_answer(i - 1)

        @pl.when(lax.rem(i, 3) == 0)
        def _():
            combine(i // 3 - lag)

        return carry

    lax.fori_loop(0, steps, step, 0)
    phase(None, 2 * steps - 1, a, b, 1)
    send_answer(steps - 1)

    def merge_rest(n, carry):
        combine(n)
        return carry

    for n in (7, 8):
        arrived(n)
    spread(6, 6)
    settle(3, 3)
    lax.fori_loop(groups - lag, groups - 1, merge_rest, 0)
    settle(4, 5)
    lax.fori_loop(groups - 1, groups + 1, merge_rest, 0)
    settle(6, 6)
    for n in range(9):
        forward(n).wait_send()

    def spread_end(p, carry):
        for kind in (2, 3):
            spread_wait(p, kind)
        for kind in range(4):
            spread_copy(p, kind).wait_send()
        return carry

    lax.fori_loop(0, 7, spread_end, 0)

    def rows_wait(n, carry):
        g = lax.rem(place + n, places)
        for h in range(2):
            remote(
                att_out.at[h, g], att_in.at[g, h], att_sent.at[h, g], att_came.at[h, g], to_head(g)
            ).wait()
        return carry

    lax.fori_loop(1, places, rows_wait, 0)

    width = 256

    def project(c, carry):
        cols = pl.ds(aligned(c, width), width)
        acc = None
        for n in range(places):
            g = lax.rem(place + n, places)
            left = jnp.concatenate([att_in[g, 0], att_in[g, 1]], 1)
            right = (w_own[:, :, cols] if n == 0 else w_all[g, :, :, cols]).reshape(
                2 * HEAD_DIM, width
            )
            term = lax.dot_general(left, right, NN, preferred_element_type=F32)
            acc = term if acc is None else acc + term
        out_ref[:, cols] = acc.astype(BF16)
        return carry

    lax.fori_loop(0, out_ref.shape[1] // width, project, 0)

    def sent_wait(n, carry):
        for source in range(2):
            @pl.when(helped[source])
            def _():
                query_copy(n, source).wait_send()

            @pl.when(asked[source])
            def _():
                answer_copy(n, source).wait_send()

        return carry

    lax.fori_loop(0, groups, sent_wait, 0)


def planned(near, shards, places, pattern, q, k, v, w):
    rows = q.shape[0]
    flat = lambda array: array.reshape(rows * 2, HEAD_DIM)
    tiles = rows // TILE
    pairs = tiles // 2
    answers = 4 * pairs
    dma = pltpu.SemaphoreType.DMA
    vm = pltpu.VMEM
    return pl.pallas_call(
        functools.partial(whole_kernel, near, shards, places),
        in_specs=[pl.BlockSpec(memory_space=pl.ANY), WHOLE] + [pl.BlockSpec(memory_space=pl.ANY)] * 3,
        out_specs=WHOLE,
        out_shape=jax.ShapeDtypeStruct((rows // places, w.shape[2]), BF16),
        scratch_shapes=[
            pltpu.SMEM((3, 2, rows // BLOCK, pattern.shape[2]), jnp.int32),
            vm((2 * rows, HEAD_DIM), BF16),
            vm((2 * rows, HEAD_DIM), BF16),
            vm(w.shape, BF16),
            dma((3,)),
            vm((2, PAIR, HEAD_DIM), F32),
            vm((2, rows, HEAD_DIM), BF16),
            vm((2, HEAD_DIM, rows), BF16),
            vm((6, rows, HEAD_DIM), BF16),
            vm((2 * pairs + answers, OUT_ROWS, PAIR), BF16),
            vm((answers, OUT_ROWS, PAIR), BF16),
            vm((rows, TILE), F32),
            vm((rows, TILE), F32),
            vm((TILE, TILE), F32),
            vm((TILE, TILE), F32),
            vm((8, TILE), F32),
            vm((8, TILE), F32),
            vm((HEAD_DIM, TILE), F32),
            vm((8, TILE), F32),
            vm((2, places, TILE, HEAD_DIM), BF16),
            vm((places, 2, TILE, HEAD_DIM), BF16),
            vm((places, 2, HEAD_DIM, w.shape[2]), BF16),
            dma((answers,)), dma((answers,)), dma((answers,)), dma((answers,)),
            dma((2, places)), dma((2, places)), dma((9,)), dma((9,)), dma((28,)), dma((28,)), dma((3,)),
        ],
        compiler_params=pltpu.CompilerParams(
            collective_id=near, has_side_effects=True, vmem_limit_bytes=VMEM_LIMIT
        ),
        name=f"whole_{near}",
    )(pattern, flat(q), flat(k), flat(v), w)


def per_device(query_states, key_states, value_states, block_pattern, helper_distances, out_weight):
    shards, places = lax.axis_size("ctx"), lax.axis_size("head")
    near = jnp.minimum(helper_distances[0], helper_distances[1])
    branches = [functools.partial(planned, r, shards, places) for r in range(1, FAR)]
    return lax.switch(
        near - 1, branches, block_pattern, query_states, key_states, value_states, out_weight
    )


def solution(mesh):
    placed = (
        P("ctx", "head", None),
        P("ctx", "head", None),
        P("ctx", "head", None),
        P("head", None, None),
        P(),
        P("head", None, None),
    )
    return jax.shard_map(
        per_device, mesh=mesh, in_specs=placed, out_specs=P(("ctx", "head"), None), check_vma=False
    )
```
